32 devices in a mesh: dp: 2 (over x), ctx: 4 (over y, core), tp: 4 (over z).
Axes of the slice: x: 2, y: 2, z: 4, core: 2. Of those that a mesh axis runs over, the one named last changes fastest.
Arguments:
- hidden_in: bfloat16 [2, 8192, 1024], P('dp', ('ctx', 'tp')), may hold values from -6 to 6
- attn_gain: bfloat16 [1024], replicated, may hold values from 0.5 to 1.5
- qkv_weight: bfloat16 [1024, 3, 1024], P(None, None, 'tp'), may hold values from -0.1875 to 0.1875
- out_weight: bfloat16 [1024, 1024], P('tp'), may hold values from -1.5 to 1.5
- mlp_gain: bfloat16 [1024], replicated, may hold values from 0.5 to 1.5
- wide_weight: bfloat16 [1024, 2, 2624], P(None, None, 'tp'), may hold values from -0.1875 to 0.1875
- down_weight: bfloat16 [2624, 1024], P('tp'), may hold values from -0.125 to 0.125
- lengths: int32 [2, 16], P('dp'), may hold values from 1 to 5120, 7680 in all within a row
- cotangent: bfloat16 [2, 8192, 1024], P('dp', ('ctx', 'tp')), may hold values from -6 to 6
Outputs:
- result: bfloat16 [2, 8192, 1024], P('dp', ('ctx', 'tp'))
- input_grad: float32 [2, 8192, 1024], P('dp', ('ctx', 'tp'))
- qkv_weight_grad: float32 [1024, 3, 1024], P(('dp', 'ctx'), None, 'tp')
- out_weight_grad: float32 [1024, 1024], P('tp', ('dp', 'ctx'))
- wide_weight_grad: float32 [1024, 2, 2624], P(('dp', 'ctx'), None, 'tp')
- down_weight_grad: float32 [2624, 1024], P('tp', ('dp', 'ctx'))
- attn_gain_grad: float32 [1024], replicated
- mlp_gain_grad: float32 [1024], replicated
The draws below stay inside these ranges and needn't reach their ends.
Inputs may be any that keep to these rules, and one draw needn't show every extreme that they name: Each row's 16 lengths sum to exactly 7680, the rest of the row being padding, and the longest is exactly 5120.
All inputs are finite; a program needn't handle non-finite values.
Results may differ from the reference program's by a relative error of at most 0.02.
Values may be sent and summed in bfloat16 or wider, within the bound.
A program may use at most 384 MiB of HBM per device.

```python
import math
from functools import partial
import jax
import jax.numpy as jnp
import numpy as np
from jax import lax

D = 1024
HEADS = 16
HD = 64
FF = 2624
NDOC = 16
ROWS = 2
LEN = 8192
DOC_MOST = 5120
QROWS = 512


def with_spikes(values, stream_key, source, target, shards_of, factor):
    def block_of(axis_at):
        return (jnp.arange(values.shape[axis_at]) // (values.shape[axis_at] // shards_of)).reshape((-1,) + (1,) * (values.ndim - 1 - axis_at))

    first = jax.random.permutation(stream_key, shards_of)[block_of(target)]
    far = (block_of(target) + shards_of // 2) % shards_of
    return jnp.where((block_of(source) == first) | (block_of(source) == far), factor * values, values)


def shard_levels(own_key, shape, cuts, low, largest):
    level = 1.0
    for axis_at, shards_of in cuts:
        draws = jax.random.uniform(jax.random.fold_in(jax.random.fold_in(own_key, 6), axis_at), (shards_of,), jnp.float32, low / len(cuts), largest / len(cuts))
        level = level * jnp.repeat(jnp.exp(draws), shape[axis_at] // shards_of).reshape((-1,) + (1,) * (len(shape) - 1 - axis_at))
    return level


def split_up(count, total, limit, slope):
    weights = [(1 << 20) // math.isqrt(rank ** slope) + 1 for rank in range(2, count + 1)]
    spare, holding = total - limit - (count - 1), [1] * (count - 1)
    while spare > 0:
        candidates = [i for i in range(count - 1) if holding[i] < limit]
        pool, remaining = sum([weights[i] for i in candidates]), spare
        for i in candidates:
            addition = min(limit - holding[i], max(1, remaining * weights[i] // pool), spare)
            holding[i] = holding[i] + addition
            spare = spare - addition
    return np.array([limit] + holding)


def uneven(rng, number_of, total, limit, slope):
    if number_of == 2:
        one = jax.random.randint(rng, (), max(1, total - limit), min(limit, total - 1) + 1)
        return jnp.stack([one, total - one])
    tallies = jnp.asarray(split_up(number_of, total, limit, slope), jnp.int32)
    pairs = (number_of - 1) // 2
    source_of, taker = tallies[1:1 + 2 * pairs:2], tallies[2:2 + 2 * pairs:2]
    margin = jnp.minimum(source_of - 1, limit - taker)
    shifted = jax.random.randint(jax.random.fold_in(rng, 1), (pairs,), 0, 1 << 20) % (margin + 1)
    tallies = tallies.at[1:1 + 2 * pairs:2].set(source_of - shifted).at[2:2 + 2 * pairs:2].set(taker + shifted)
    return tallies[jax.random.permutation(jax.random.fold_in(rng, 2), number_of)]


def bell_draw(own_key, dims, deviation, most, pieces=(), held_as=jnp.bfloat16):
    array = jax.random.normal(own_key, dims, jnp.float32) * deviation
    if len(pieces) > 0:
        array = shard_levels(own_key, dims, pieces, -0.22, 0.18) * array
    return jnp.clip(array, min=-most, max=most).astype(held_as)


def noise_with(rng, shape, deviation, limit, cuts, heavy, kind=jnp.bfloat16):
    array = deviation * jax.random.normal(rng, shape, jnp.float32)
    if cuts:
        array = array * shard_levels(rng, shape, cuts, -0.22, 0.18)
    return jnp.clip(with_spikes(array, jax.random.fold_in(rng, 3), *heavy), -limit, limit).astype(kind)


def setup_inputs(seed: int = 0) -> dict:
    keys = jax.random.split(jax.random.key(seed), 10)
    hidden_in = bell_draw(keys[0], (ROWS, LEN, D), 1.0, 6.0, ((0, 2), (1, 16)))
    attn_gain = jnp.clip(1.0 + 0.1 * jax.random.normal(keys[1], (D,), jnp.float32), 0.5, 1.5).astype(jnp.bfloat16)
    qkv_weight = bell_draw(keys[2], (D, 3, D), D ** -0.5, 0.1875, ((2, 4),))
    out_weight = bell_draw(keys[3], (D, D), (D // 64) ** -0.5, 1.5, ((0, 4),))
    mlp_gain = jnp.clip(1.0 + 0.1 * jax.random.normal(keys[4], (D,), jnp.float32), 0.5, 1.5).astype(jnp.bfloat16)
    wide_weight = bell_draw(keys[5], (D, 2, FF), D ** -0.5, 0.1875, ((2, 4),))
    down_weight = bell_draw(keys[6], (FF, D), FF ** -0.5, 0.125, ((0, 4),))
    lengths = jax.vmap(lambda own: uneven(own, NDOC, LEN * 15 // 16, DOC_MOST, 2))(jax.random.split(keys[7], ROWS)).reshape((ROWS, NDOC)).astype(jnp.int32)
    cotangent = noise_with(keys[8], (ROWS, LEN, D), 1.0, 6.0, ((0, 2), (1, 16)), (1, 2, 16, 2.0))
    return dict(hidden_in=hidden_in, attn_gain=attn_gain, qkv_weight=qkv_weight, out_weight=out_weight, mlp_gain=mlp_gain, wide_weight=wide_weight, down_weight=down_weight, lengths=lengths, cotangent=cotangent)


eps_norm = 1e-05
theta_base = 160000.0
neg_fill = -1e+30

@jax.custom_vjp
def low(v):
    return lax.optimization_barrier(v.astype(jnp.bfloat16)).astype(jnp.float32)

@jax.custom_vjp
def low_back(v):
    return v

def low_keep(v):
    return (low(v), None)

def low_pass(kept, grad):
    return (grad,)

def back_keep(v):
    return (v, None)

def back_low(kept, grad):
    return (low(grad),)
low.defvjp(low_keep, low_pass)
low_back.defvjp(back_keep, back_low)

def layout(length_row, row_length):
    doc_count = length_row.shape[0]
    doc_ends = jnp.cumsum(length_row).astype(jnp.int32)
    starts = (doc_ends - length_row).astype(jnp.int32)
    places = lax.iota(jnp.int32, row_length)
    segment = lax.optimization_barrier(jnp.sum((places[:, None] >= doc_ends[None, :]).astype(jnp.int32), axis=1)).astype(jnp.int32)
    owned = segment[:, None] == lax.iota(jnp.int32, doc_count)[None, :]
    offset = lax.optimization_barrier(jnp.sum(jnp.where(owned, starts[None, :], 0), axis=1)).astype(jnp.int32)
    filled_to = doc_ends[doc_count - 1]
    offset = jnp.where(segment == doc_count, filled_to, offset)
    return (segment, (places - offset).astype(jnp.int32), places < filled_to)

def normalize(row_values, norm_gain):
    row_mean = lax.optimization_barrier(jnp.mean(row_values, axis=-1, keepdims=True))
    centered = row_values - row_mean
    variance = lax.optimization_barrier(jnp.mean(centered * centered, axis=-1, keepdims=True))
    return centered * lax.rsqrt(variance + eps_norm) * norm_gain

def rotate(field_in, in_doc, head_count):
    half_size = HD // 2
    frequency = jnp.exp(lax.iota(jnp.float32, half_size) * (-2.0 * math.log(theta_base) / HD))
    angles = in_doc.astype(jnp.float32)[..., None] * frequency
    cosine = jnp.cos(angles)[..., None, :]
    sine_part = jnp.sin(angles)[..., None, :]
    shaped = field_in.reshape(field_in.shape[:-1] + (head_count, HD))
    first_half = shaped[..., :half_size]
    second = shaped[..., half_size:]
    turned = jnp.concatenate([first_half * cosine - second * sine_part, second * cosine + first_half * sine_part], axis=-1)
    return turned.reshape(field_in.shape)

def geglu(gate_in, up_in):
    return jax.nn.gelu(gate_in, approximate=False) * up_in

def reference(hidden_in, attn_gain, qkv_weight, out_weight, mlp_gain, wide_weight, down_weight, lengths, cotangent):
    segment, in_doc, filled = jax.vmap(partial(layout, row_length=LEN))(lengths)
    score_scale = 1.0 / math.sqrt(HD)
    highest = lax.Precision.HIGHEST

    def attend_row(packed):
        query_row, key_row, value_row, seg_row = packed
        block_count = LEN // QROWS
        key_heads = key_row.reshape(LEN, HEADS, HD)
        value_heads = value_row.reshape(LEN, HEADS, HD)

        def attend_block(block):
            query_block, seg_block = block
            scores = jnp.einsum('qhd,khd->hqk', query_block, key_heads, precision=highest) * score_scale
            scores = low_back(scores)
            allowed = (seg_block[:, None] == seg_row[None, :])[None]
            masked = jnp.where(allowed, scores, neg_fill)
            row_peak = lax.optimization_barrier(jnp.max(masked, axis=-1, keepdims=True))
            log_total = row_peak + jnp.log(lax.optimization_barrier(jnp.sum(jnp.exp(masked - row_peak), axis=-1, keepdims=True)))
            weights = low(jnp.exp(masked - log_total))
            return jnp.einsum('hqk,khd->qhd', weights, value_heads, precision=highest)
        outputs = lax.map(jax.checkpoint(attend_block), (query_row.reshape(block_count, QROWS, HEADS, HD), seg_row.reshape(block_count, QROWS)))
        return outputs.reshape(LEN, D)

    def forward(inputs, gain_one, qkv_mat, out_mat, gain_two, wide_mat, down_mat):
        normed = low(normalize(inputs, gain_one))
        mixed_cols = jnp.einsum('rtd,dcf->rtcf', normed, qkv_mat, precision=highest)
        queries = low(rotate(low_back(mixed_cols[:, :, 0]), in_doc, HEADS))
        key_rows = low(rotate(low_back(mixed_cols[:, :, 1]), in_doc, HEADS))
        value_rows = low(low_back(mixed_cols[:, :, 2]))
        attended = lax.map(attend_row, (queries, key_rows, value_rows, segment))
        attended = low(low_back(attended))
        branch = low_back(jnp.einsum('rtf,fd->rtd', attended, out_mat, precision=highest))
        middle = inputs + branch
        normed_two = low(normalize(middle, gain_two))
        wide_cols = low_back(jnp.einsum('rtd,dcf->rtcf', normed_two, wide_mat, precision=highest))
        product = low(geglu(wide_cols[:, :, 0], wide_cols[:, :, 1]))
        mlp_out = low_back(jnp.einsum('rtf,fd->rtd', product, down_mat, precision=highest))
        return jnp.where(filled[:, :, None], middle + mlp_out, 0.0)
    result, pull_back = jax.vjp(forward, hidden_in.astype(jnp.float32), attn_gain.astype(jnp.float32), qkv_weight.astype(jnp.float32), out_weight.astype(jnp.float32), mlp_gain.astype(jnp.float32), wide_weight.astype(jnp.float32), down_weight.astype(jnp.float32))
    gradients = pull_back(cotangent.astype(jnp.float32))
    return (result.astype(jnp.bfloat16), gradients[0], gradients[2], gradients[3], gradients[5], gradients[6], gradients[1], gradients[4])
```

```python
from functools import partial
import math

import jax
import jax.numpy as jnp
from jax import lax
from jax.experimental import pallas as pl
from jax.experimental.pallas import tpu as pltpu
from jax.sharding import PartitionSpec as P

HD = 64
HALF = HD // 2
EPS = 1e-05
THETA = 160000.0
NEG = -1e30
LOG2E = 1.4426950408889634
LN2 = 0.6931471805599453
BF = jnp.bfloat16
F32 = jnp.float32
ROWS_V = HD + 16


def dot(a, b, dims):
    return lax.dot_general(a, b, (dims, ((), ())), preferred_element_type=F32)


def layout(length_row, row_length):
    count = length_row.shape[0]
    order = lax.iota(jnp.int32, count)
    ends = jnp.sum(jnp.where(order[:, None] <= order[None, :], length_row[:, None], 0), axis=0)
    places = lax.iota(jnp.int32, row_length)
    passed = places[:, None] >= ends[None, :]
    start = jnp.max(jnp.where(passed, ends[None, :], 0), axis=1)
    end = jnp.min(jnp.where(passed, row_length, ends[None, :]), axis=1)
    return start, end, ends[count - 1]


def ranges(q_start, q_end, rows, keys):
    first = q_start.reshape(-1, rows)[:, 0]
    last = q_end.reshape(-1, rows)[:, -1]
    first_end = q_end.reshape(-1, rows)[:, 0]
    lo = first // keys
    hi = (last + keys - 1) // keys
    flo = (first + keys - 1) // keys
    fhi = last // keys
    plain = (first_end == last) & (fhi > flo)
    return jnp.stack([lo, hi, jnp.where(plain, flo, hi), jnp.where(plain, fhi, hi)])


def normalize(values, gain):
    mean = jnp.mean(values, axis=-1, keepdims=True)
    centered = values - mean
    inverse = lax.rsqrt(jnp.mean(centered * centered, axis=-1, keepdims=True) + EPS)
    return centered * inverse * gain, centered, inverse


def normalize_back(grad, centered, inverse, gain):
    scaled = grad * gain
    shift = jnp.mean(scaled, axis=-1, keepdims=True)
    along = jnp.mean(scaled * centered, axis=-1, keepdims=True)
    back = inverse * (scaled - shift) - centered * (inverse * inverse * inverse * along)
    return back, jnp.sum(grad * centered * inverse, axis=0)


def allowed(block, keys, start, end):
    at = block * keys + lax.broadcasted_iota(jnp.int32, (keys, 1), 0)
    return (at >= start) & (at < end)


def prepare(source, target):
    chunk = source.shape[-1]
    for c in range(source.shape[0]):
        target[pl.ds(c * chunk, chunk), :] = source[c, 0, 0].astype(F32).T.astype(BF)


def forward_kernel(keys, table, start_ref, end_ref, q_ref, k_ref, v_ref, o_ref, lse_ref, k_rows, v_cols):
    i = pl.program_id(1)
    chunk = k_ref.shape[-1]

    @pl.when(i == 0)
    def _():
        prepare(k_ref, k_rows)
        for c in range(k_ref.shape[0]):
            at = pl.ds(c * chunk, chunk)
            v_cols[:HD, at] = v_ref[c, 0, 0]
            ones = lax.broadcasted_iota(jnp.int32, (ROWS_V - HD, chunk), 0) == 0
            v_cols[HD:, at] = jnp.where(ones, 1.0, 0.0).astype(BF)

    q = q_ref[0, 0, 0]
    rows = q.shape[1]
    start, end = start_ref[...], end_ref[...]

    def step(masked, block, carry):
        peak, total = carry
        at = pl.multiple_of(block * keys, keys)
        scores = dot(k_rows[pl.ds(at, keys), :], q, ((1,), (0,)))
        if masked:
            scores = jnp.where(allowed(block, keys, start, end), scores, NEG)
        new_peak = jnp.maximum(peak, jnp.max(scores, axis=0, keepdims=True))
        weights = jnp.exp2(scores - new_peak).astype(BF)
        total = total * jnp.exp2(peak - new_peak) + dot(v_cols[:, pl.ds(at, keys)], weights, ((1,), (0,)))
        return new_peak, total

    carry = (jnp.full((1, rows), NEG, F32), jnp.zeros((ROWS_V, rows), F32))
    lo, hi, flo, fhi = (table[j, i] for j in range(4))
    carry = lax.fori_loop(lo, flo, partial(step, True), carry)
    carry = lax.fori_loop(flo, fhi, partial(step, False), carry)
    peak, total = lax.fori_loop(fhi, hi, partial(step, True), carry)
    weight = total[HD : HD + 1]
    o_ref[0, 0] = (total[:HD] / weight).astype(BF)
    lse_ref[0] = peak + jnp.log2(weight)


def attend(table, start, end, q, k, v, share, rows, keys):
    (q, qj), (k, kj), (v, vj) = q, k, v
    q_chunks, _, heads, _, chunk = q.shape
    k_chunks = k.shape[0]
    tokens = q_chunks * chunk
    per_chunk, per_share = chunk // rows, share // rows
    row_spec = pl.BlockSpec((1, rows), lambda h, i, t: (0, i))
    whole = (k_chunks, 1, 1, HD, chunk)
    return pl.pallas_call(
        partial(forward_kernel, keys),
        out_shape=(
            jax.ShapeDtypeStruct((tokens // share, heads, HD, share), BF),
            jax.ShapeDtypeStruct((heads, 1, tokens), F32),
        ),
        grid_spec=pltpu.PrefetchScalarGridSpec(
            num_scalar_prefetch=1,
            grid=(heads, tokens // rows),
            in_specs=[
                row_spec,
                row_spec,
                pl.BlockSpec((1, 1, 1, HD, rows), lambda h, i, t: (i // per_chunk, qj, h, 0, i % per_chunk)),
                pl.BlockSpec(whole, lambda h, i, t: (0, kj, h, 0, 0)),
                pl.BlockSpec(whole, lambda h, i, t: (0, vj, h, 0, 0)),
            ],
            out_specs=[
                pl.BlockSpec((1, 1, HD, rows), lambda h, i, t: (i // per_share, h, 0, i % per_share)),
                pl.BlockSpec((1, 1, rows), lambda h, i, t: (h, 0, i)),
            ],
            scratch_shapes=[
                pltpu.VMEM((k_chunks * chunk, HD), BF),
                pltpu.VMEM((ROWS_V, k_chunks * chunk), BF),
            ],
        ),
        compiler_params=pltpu.CompilerParams(vmem_limit_bytes=48 << 20),
        name="attend",
    )(table, start, end, q, k, v)


def backward_kernel(
    keys, scale, table, start_ref, end_ref, lse_ref, q_ref, k_ref, v_ref, o_ref, g_ref, dq_ref, dkv_ref,
    k_rows, v_rows, dk_sum, dv_sum,
):
    i = pl.program_id(1)
    chunk = k_ref.shape[-1]
    per_chunk = chunk // keys

    @pl.when(i == 0)
    def _():
        prepare(k_ref, k_rows)
        prepare(v_ref, v_rows)
        dk_sum[...] = jnp.zeros_like(dk_sum)
        dv_sum[...] = jnp.zeros_like(dv_sum)

    q, g = q_ref[0, 0, 0], g_ref[0, 0]
    rows = q.shape[1]
    q_rows, g_rows = q.astype(F32).T.astype(BF), g.astype(F32).T.astype(BF)
    delta = jnp.sum(g.astype(F32) * o_ref[0, 0].astype(F32), axis=0, keepdims=True)
    lse = lse_ref[0]
    start, end = start_ref[...], end_ref[...]

    def step(masked, block, dq):
        at = pl.multiple_of(block * keys, keys)
        here = pl.ds(at, keys)
        probs = jnp.exp2(dot(k_rows[here, :], q, ((1,), (0,))) - lse)
        if masked:
            probs = jnp.where(allowed(block, keys, start, end), probs, 0.0)
        d_probs = dot(v_rows[here, :], g, ((1,), (0,)))
        d_scores = (probs * (d_probs - delta)).astype(BF)
        dv_sum[here, :] += dot(probs.astype(BF), g_rows, ((1,), (0,)))
        dk_sum[here, :] += dot(d_scores, q_rows, ((1,), (0,)))
        columns = pl.ds(pl.multiple_of((block % per_chunk) * keys, keys), keys)
        return dq + dot(k_ref[block // per_chunk, 0, 0, :, columns], d_scores, ((1,), (0,)))

    lo, hi, flo, fhi = (table[j, i] for j in range(4))
    dq = jnp.zeros((HD, rows), F32)
    dq = lax.fori_loop(lo, flo, partial(step, True), dq)
    dq = lax.fori_loop(flo, fhi, partial(step, False), dq)
    dq = lax.fori_loop(fhi, hi, partial(step, True), dq)
    dq_ref[0, 0] = (dq * scale).astype(BF)

    @pl.when(i == pl.num_programs(1) - 1)
    def _():
        for c in range(k_ref.shape[0]):
            at = pl.ds(c * chunk, chunk)
            dkv_ref[c, 0, 0] = (dk_sum[at, :].T * LN2).astype(BF)
            dkv_ref[c, 1, 0] = dv_sum[at, :].T.astype(BF)


def attend_back(table, start, end, lse, q, k, v, out, grad, share, rows, keys, scale):
    (q, qj), (k, kj), (v, vj) = q, k, v
    q_chunks, _, heads, _, chunk = q.shape
    k_chunks = k.shape[0]
    tokens = q_chunks * chunk
    per_chunk, per_share = chunk // rows, share // rows
    row_spec = pl.BlockSpec((1, rows), lambda h, i, t: (0, i))
    whole = (k_chunks, 1, 1, HD, chunk)
    share_spec = pl.BlockSpec((1, 1, HD, rows), lambda h, i, t: (i // per_share, h, 0, i % per_share))
    return pl.pallas_call(
        partial(backward_kernel, keys, scale),
        out_shape=(
            jax.ShapeDtypeStruct((q_chunks, heads, HD, chunk), BF),
            jax.ShapeDtypeStruct((k_chunks, 2, heads, HD, chunk), BF),
        ),
        grid_spec=pltpu.PrefetchScalarGridSpec(
            num_scalar_prefetch=1,
            grid=(heads, tokens // rows),
            in_specs=[
                row_spec,
                row_spec,
                pl.BlockSpec((1, 1, rows), lambda h, i, t: (h, 0, i)),
                pl.BlockSpec((1, 1, 1, HD, rows), lambda h, i, t: (i // per_chunk, qj, h, 0, i % per_chunk)),
                pl.BlockSpec(whole, lambda h, i, t: (0, kj, h, 0, 0)),
                pl.BlockSpec(whole, lambda h, i, t: (0, vj, h, 0, 0)),
                share_spec,
                share_spec,
            ],
            out_specs=[
                pl.BlockSpec((1, 1, HD, rows), lambda h, i, t: (i // per_chunk, h, 0, i % per_chunk)),
                pl.BlockSpec((k_chunks, 2, 1, HD, chunk), lambda h, i, t: (0, 0, h, 0, 0)),
            ],
            scratch_shapes=[
                pltpu.VMEM((k_chunks * chunk, HD), BF),
                pltpu.VMEM((k_chunks * chunk, HD), BF),
                pltpu.VMEM((k_chunks * chunk, HD), F32),
                pltpu.VMEM((k_chunks * chunk, HD), F32),
            ],
        ),
        compiler_params=pltpu.CompilerParams(vmem_limit_bytes=56 << 20),
        name="attend_back",
    )(table, start, end, lse, q, k, v, out, grad)


def turn(pairs, cosine, sine):
    a, b = pairs[..., 0, :, :], pairs[..., 1, :, :]
    return jnp.stack([a * cosine - b * sine, b * cosine + a * sine], axis=-3)


def gelu_parts(gate):
    lower = 0.5 * (1.0 + lax.erf(gate * math.sqrt(0.5)))
    slope = lower + gate * (jnp.exp(-0.5 * gate * gate) * (1.0 / math.sqrt(2.0 * math.pi)))
    return gate * lower, slope


def body(hidden_in, attn_gain, qkv_weight, out_weight, mlp_gain, wide_weight, down_weight, lengths, cotangent):
    share, width = hidden_in.shape[1:]
    ctx, tp = lax.axis_size("ctx"), lax.axis_size("tp")
    copies = lax.axis_size("dp") * ctx
    group = share * tp
    length = group * ctx
    heads = qkv_weight.shape[2] // HD
    units = down_weight.shape[0]
    part = width // copies
    scale = 1.0 / math.sqrt(HD)
    copy_at = lax.axis_index("dp") * ctx + lax.axis_index("ctx")
    everywhere, reduced = ("tp", "dp", "ctx"), ("dp", "ctx")

    def rows_of(array, dim):
        size = array.shape[dim] // copies
        return lax.dynamic_slice_in_dim(array, copy_at * size, size, dim)

    def gather(array):
        return lax.all_gather(array, everywhere, axis=0, tiled=True)

    start, end, filled_to = layout(lengths[0], length)
    group_at = lax.axis_index("ctx") * group
    share_at = group_at + lax.axis_index("tp") * share
    live = (share_at + lax.iota(jnp.int32, share) < filled_to)[:, None]
    places = group_at + lax.iota(jnp.int32, group)
    in_doc = places - lax.dynamic_slice_in_dim(start, group_at, group)
    frequency = jnp.exp(lax.iota(F32, HALF) * (-2.0 * math.log(THETA) / HD))
    angles = frequency[:, None] * in_doc.astype(F32)[None, :]
    cosine, sine = jnp.cos(angles), jnp.sin(angles)

    inputs = hidden_in[0].astype(F32)
    gain_one, gain_two = attn_gain.astype(F32), mlp_gain.astype(F32)
    normed, centered, inverse = normalize(inputs, gain_one)
    normed_full = lax.all_gather(normed.astype(BF), "tp", axis=0, tiled=True)

    out_full = gather(rows_of(out_weight, 0))
    wide_full = gather(rows_of(wide_weight, 0).reshape(part, 2 * units)).reshape(tp, width, 2 * units)
    down_full = gather(rows_of(down_weight, 1).T).reshape(tp, width, units)

    mixed = dot(qkv_weight.reshape(width, 3 * heads * HD), normed_full, ((0,), (1,)))
    mixed = mixed.reshape(3, heads, 2, HALF, group)
    mixed = jnp.stack(
        [
            turn(mixed[0], cosine, sine) * (scale * LOG2E),
            turn(mixed[1], cosine, sine),
            mixed[2],
        ]
    ).astype(BF)

    spread = heads % ctx == 0
    rows = min(512, share)
    if spread:
        own = heads // ctx
        mixed = mixed.reshape(3, ctx, own, HD, group).transpose(1, 0, 2, 3, 4)
        mixed = lax.all_to_all(mixed, "ctx", 0, 0, tiled=True)
        queries, key_side, value_side = (mixed, 0), (mixed, 1), (mixed, 2)
        q_start, q_end = start, end
    else:
        mixed = mixed.reshape(3, heads, HD, group)
        both = lax.all_gather(mixed[1:], "ctx", axis=0)
        queries, key_side, value_side = (mixed[:1][None], 0), (both, 0), (both, 1)
        q_start = lax.dynamic_slice_in_dim(start, group_at, group)
        q_end = lax.dynamic_slice_in_dim(end, group_at, group)
    keys = 512
    table = ranges(q_start, q_end, rows, keys)
    q_start, q_end = q_start[None], q_end[None]
    shares, lse = attend(table, q_start, q_end, queries, key_side, value_side, share, rows, keys)
    if spread:
        attended = lax.all_to_all(shares, ("ctx", "tp"), 0, 0, tiled=True)
        attended = attended.reshape(ctx, tp, own * HD, share).transpose(1, 0, 2, 3)
    else:
        attended = lax.all_to_all(shares, "tp", 0, 0, tiled=True)
    attended = attended.reshape(width, share)

    middle = inputs + dot(attended, out_full, ((0,), (0,)))
    normed_two, centered_two, inverse_two = normalize(middle, gain_two)
    normed_two = normed_two.astype(BF)
    grad = jnp.where(live, cotangent[0], jnp.zeros_like(cotangent[0]))
    mlp_out = jnp.zeros((share, width), F32)
    d_normed_two = jnp.zeros((share, width), F32)
    products, d_wides = [], []
    for s in range(tp):
        wide = dot(normed_two, wide_full[s], ((1,), (0,)))
        up = wide[:, units:]
        active, slope = gelu_parts(wide[:, :units])
        product = (active * up).astype(BF)
        d_product = dot(grad, down_full[s], ((1,), (0,)))
        d_wide = jnp.concatenate([d_product * up * slope, d_product * active], axis=1).astype(BF)
        mlp_out = mlp_out + dot(product, down_full[s], ((1,), (1,)))
        d_normed_two = d_normed_two + dot(d_wide, wide_full[s], ((1,), (1,)))
        products.append(product)
        d_wides.append(d_wide)
    product, d_wide = jnp.concatenate(products, axis=1), jnp.concatenate(d_wides, axis=1)
    result = jnp.where(live, middle + mlp_out, 0.0).astype(BF)
    back_two, gain_two_grad = normalize_back(d_normed_two, centered_two, inverse_two, gain_two)
    d_middle = grad.astype(F32) + back_two
    d_branch = d_middle.astype(BF)
    d_attended = dot(out_full, d_branch, ((1,), (1,))).astype(BF)

    wide_grad = dot(normed_two, d_wide, ((0,), (0,))).astype(BF)
    down_grad = dot(grad, product, ((0,), (0,))).astype(BF)
    out_grad = dot(d_branch, attended, ((0,), (1,))).astype(BF)

    def reduce(partial_sum):
        mine = lax.psum_scatter(partial_sum, reduced, scatter_dimension=0, tiled=True)
        mine = mine.reshape(part, tp, -1).transpose(1, 0, 2)
        return lax.psum_scatter(mine, "tp", scatter_dimension=0, tiled=False).astype(F32)

    wide_part = reduce(wide_grad).reshape(part, 2, units)
    down_part = reduce(down_grad).T
    out_part = reduce(out_grad).T

    if spread:
        d_shares = d_attended.reshape(tp, ctx, own * HD, share).transpose(1, 0, 2, 3)
        d_shares = d_shares.reshape(tp * ctx, own, HD, share)
        d_shares = lax.all_to_all(d_shares, ("ctx", "tp"), 0, 0, tiled=True)
    else:
        d_shares = lax.all_to_all(d_attended.reshape(tp, heads, HD, share), "tp", 0, 0, tiled=True)
    dq, dkv = attend_back(
        table, q_start, q_end, lse, queries, key_side, value_side, shares, d_shares, share, rows, keys, scale
    )
    if spread:
        d_mixed = jnp.concatenate([dq[:, None], dkv], axis=1)
        d_mixed = lax.all_to_all(d_mixed, "ctx", 0, 0, tiled=True)
        d_mixed = d_mixed.transpose(1, 0, 2, 3, 4)
    else:
        dkv = lax.psum_scatter(dkv, "ctx", scatter_dimension=0, tiled=False)
        d_mixed = jnp.concatenate([dq, dkv], axis=0)
    d_mixed = d_mixed.reshape(3, heads, 2, HALF, group).astype(F32)
    d_mixed = jnp.stack([turn(d_mixed[0], cosine, -sine), turn(d_mixed[1], cosine, -sine), d_mixed[2]])
    d_mixed = d_mixed.astype(BF).reshape(3 * heads * HD, group)
    qkv_grad = dot(normed_full, d_mixed, ((0,), (1,))).astype(BF)
    d_normed = dot(d_mixed, qkv_weight.reshape(width, 3 * heads * HD), ((0,), (1,))).astype(BF)
    d_normed = lax.psum_scatter(d_normed, "tp", scatter_dimension=0, tiled=True).astype(F32)
    qkv_part = lax.psum_scatter(qkv_grad, reduced, scatter_dimension=0, tiled=True).astype(F32)
    qkv_part = qkv_part.reshape(part, 3, heads * HD)
    back_one, gain_one_grad = normalize_back(d_normed, centered, inverse, gain_one)
    input_grad = d_middle + back_one
    gain_one_sum, gain_two_sum = lax.psum((gain_one_grad, gain_two_grad), ("dp", "ctx", "tp"))
    return (
        result[None],
        input_grad[None],
        qkv_part,
        out_part,
        wide_part,
        down_part,
        gain_one_sum,
        gain_two_sum,
    )


def solution(mesh):
    tokens = P("dp", ("ctx", "tp"), None)
    placed = (tokens, P(), P(None, None, "tp"), P("tp", None), P(), P(None, None, "tp"), P("tp", None), P("dp", None), tokens)
    return jax.shard_map(
        body,
        mesh=mesh,
        in_specs=placed,
        out_specs=(
            tokens,
            tokens,
            P(("dp", "ctx"), None, "tp"),
            P("tp", ("dp", "ctx")),
            P(("dp", "ctx"), None, "tp"),
            P("tp", ("dp", "ctx")),
            P(),
            P(),
        ),
        check_vma=False,
    )
```
